128 devices in a mesh: dp: 2 (over core), expert: 64 (over y, z, x).
Axes of the slice: x: 4, y: 4, z: 4, core: 2. Of those that a mesh axis runs over, the one named last changes fastest.
Arguments:
- tokens: bfloat16 [16384, 4096], P(('dp', 'expert')), parts along dimension 0, may hold values from -6 to 6
- w_gate_up: bfloat16 [64, 2, 4096, 768], P('expert'), may hold values from -0.09375 to 0.09375
- w_down: bfloat16 [64, 768, 4096], P('expert'), may hold values from -0.21875 to 0.21875
- routes: int32 [16384, 8], P(('dp', 'expert')), parts along dimension 0, may hold values from 0 to 63, as said below
- gate_scaled: int32 [16384, 8], P(('dp', 'expert')), parts along dimension 0, may hold values from 1 to 1023
Outputs:
- mixed: bfloat16 [16384, 4096], P(('dp', 'expert')), parts along dimension 0
The draws below stay inside these ranges and needn't reach their ends.
There are 2 independent parts, one for each index of `dp`. The reference program is written for one: setup_inputs(seed, part) draws one part's arguments, and reference() takes and returns one part's arrays. A program takes and returns all parts, laid end to end along the dimension named above; an argument that names none is the same for every part. Nothing has to cross between parts.
Inputs may be any that keep to these rules, and one draw needn't show every extreme that they name: `routes`: every row names 8 different experts. In each aligned block of 128 rows (the rows of one device) one expert, the same in every block, is named by exactly 40 rows; no other expert is named by more than 20 rows of a block, and a second expert, the same in every block, by exactly 20 rows of every block.
All inputs are finite; a program needn't handle non-finite values.
Results may differ from the reference program's by a relative error of at most 0.0057.
Values may be sent and summed in bfloat16 or wider, within the bound.
No kernel may reach another device: no remote copies, remote signals or barrier semaphores. Data moves between devices by JAX's collectives and lax.ppermute only.
A program may use at most 192 MiB of HBM per device.

```python
import jax
import jax.numpy as jnp
from jax import lax

D = 4096
FFW = 768
TOP = 8
TOK_DEV = 128
EXPERTS = 64
TOKENS = 8192
COLD = 20
MOST = 40
N_EXPERT = 64


def draw_routes(key, part):
    blocks = TOKENS // TOK_DEV
    labels = jax.random.permutation(jax.random.fold_in(key, 11), EXPERTS).astype(jnp.int32)
    remaining = TOK_DEV * TOP - MOST - COLD

    def shuffle_row(row_key):
        return jax.random.permutation(row_key, TOP)

    def one_block(block_index):
        block_key = jax.random.fold_in(key, block_index)
        capacity_units = jax.random.permutation(jax.random.fold_in(block_key, 1), (EXPERTS - 2) * COLD)
        chosen = (capacity_units < remaining).astype(jnp.int32).reshape(EXPERTS - 2, COLD)
        counts = jnp.concatenate([jnp.array([MOST, COLD], jnp.int32), jnp.sum(chosen, axis=1).astype(jnp.int32)])
        listed = jnp.repeat(labels, counts, total_repeat_length=TOK_DEV * TOP)
        assigned = listed.reshape(TOP, TOK_DEV).T
        row_order = jax.random.permutation(jax.random.fold_in(block_key, 2), TOK_DEV)
        assigned = assigned[row_order]
        column_keys = jax.random.split(jax.random.fold_in(block_key, 3), TOK_DEV)
        column_orders = jax.vmap(shuffle_row)(column_keys)
        return jnp.take_along_axis(assigned, column_orders, axis=1)
    return jax.vmap(one_block)(jnp.arange(blocks)).reshape(TOKENS, TOP).astype(jnp.int32)


def plant(values, key, smallest, high):
    index_at = [jax.random.randint(jax.random.fold_in(key, axis), (), 0, length) for axis, length in enumerate(values.shape)]
    widest = values.shape.index(max(values.shape))
    neighbour = index_at[:widest] + [(index_at[widest] + 1) % values.shape[widest]] + index_at[widest + 1:]
    return values.at[tuple(index_at)].set(smallest).at[tuple(neighbour)].set(high)


def block_levels(own_key, extent, shards, smallest, top_value):
    loudness, own = 1.0, jax.random.fold_in(own_key, 6)
    for position, blocks in shards:
        draws = jnp.exp(jax.random.uniform(jax.random.fold_in(own, position), (blocks,), jnp.float32, smallest / len(shards), top_value / len(shards)))
        loudness = loudness * jnp.repeat(draws, extent[position] // blocks).reshape([-1 if axis == position else 1 for axis in range(len(extent))])
    return loudness


def bell_draw(key, dims, scale, bound, cuts=(), held_as=jnp.bfloat16):
    values = jax.random.normal(key, dims, jnp.float32) * scale
    if len(cuts) > 0:
        values = block_levels(key, dims, cuts, -0.22, 0.18) * values
    return jnp.clip(values, min=-bound, max=bound).astype(held_as)


def setup_inputs(seed: int = 0, part: int = 0) -> dict:
    keys = jax.random.split(jax.random.key(seed), 6)
    part_keys = jax.random.split(jax.random.fold_in(keys[5], part), 6)
    return {
        "tokens": bell_draw(part_keys[0], (TOKENS, D), 1.0, 6.0, ((0, 64),)),
        "w_gate_up": bell_draw(keys[1], (EXPERTS, 2, D, FFW), D ** -0.5, 0.09375, ((0, 64),)),
        "w_down": bell_draw(keys[2], (EXPERTS, FFW, D), FFW ** -0.5, 0.21875, ((0, 64),)),
        "routes": draw_routes(jax.random.fold_in(jax.random.fold_in(keys[5], part), 71), part),
        "gate_scaled": plant(jax.random.randint(part_keys[4], (TOKENS, TOP), 1, 1024), jax.random.fold_in(part_keys[4], 1), 1, 1023).astype(jnp.int32),
    }


def expert_rows(picked, gate_up, down_proj):
    gate_val = jnp.dot(picked, gate_up[0], preferred_element_type=jnp.float32)
    up_val = jnp.dot(picked, gate_up[1], preferred_element_type=jnp.float32)
    hidden = (jax.nn.silu(gate_val) * up_val).astype(jnp.bfloat16)
    return jnp.dot(hidden, down_proj, preferred_element_type=jnp.float32).astype(jnp.bfloat16)


def reference(tokens, w_gate_up, w_down, routes, gate_scaled):
    slot_total = TOKENS * TOP
    flat_routes = routes.reshape(-1)
    capacity = N_EXPERT * MOST

    def per_expert(carry, expert):
        indices = jnp.nonzero(flat_routes == expert, size=capacity, fill_value=slot_total)[0].astype(jnp.int32)
        token_index = jnp.minimum(indices // TOP, TOKENS - 1).astype(jnp.int32)
        picked = jnp.take(tokens, token_index, axis=0)
        gate_up = lax.dynamic_index_in_dim(w_gate_up, expert, 0, keepdims=False)
        down_proj = lax.dynamic_index_in_dim(w_down, expert, 0, keepdims=False)
        results = expert_rows(picked, gate_up, down_proj)
        return carry.at[indices].set(results, mode="drop"), None

    filled, _ = lax.scan(per_expert, jnp.zeros((slot_total, D), jnp.bfloat16), jnp.arange(EXPERTS, dtype=jnp.int32))
    scaled = gate_scaled.astype(jnp.float32)
    weight = scaled / jnp.sum(scaled, axis=1, keepdims=True)
    mixed = jnp.einsum("tk,tkd->td", weight, filled.reshape(TOKENS, TOP, D).astype(jnp.float32))
    return mixed.astype(jnp.bfloat16)
```

```python
import jax
import jax.numpy as jnp
from jax import lax
from jax.sharding import PartitionSpec as P

def expert_sums(picked, gate, up, down):
    gate_val = jnp.dot(picked, gate, preferred_element_type=jnp.float32)
    up_val = jnp.dot(picked, up, preferred_element_type=jnp.float32)
    hidden = (jax.nn.silu(gate_val) * up_val).astype(jnp.bfloat16)
    return jnp.dot(hidden, down, preferred_element_type=jnp.float32)


def body(tokens, w_gate_up, w_down, routes, gate_scaled):
    experts = lax.axis_size("expert")
    tok_rows, width = tokens.shape
    slots = 24
    gate, up, down = w_gate_up[0, 0], w_gate_up[0, 1], w_down[0]

    routes_t = routes.T
    expert_ids = jnp.arange(experts, dtype=jnp.int32)
    hit = routes_t[:, None, :] == expert_ids[None, :, None]
    named = jnp.any(hit, axis=0)
    earlier = jnp.arange(tok_rows)[:, None] < jnp.arange(tok_rows)[None, :]
    rank = jnp.dot(
        named.astype(jnp.bfloat16), earlier.astype(jnp.bfloat16), preferred_element_type=jnp.float32
    ).astype(jnp.int32)
    counts = jnp.sum(named.astype(jnp.int32), axis=1)
    busiest = jnp.argmax(counts).astype(jnp.int32)
    scaled = gate_scaled.T.astype(jnp.float32)
    weight = scaled / jnp.sum(scaled, axis=0, keepdims=True)
    weight_of = jnp.sum(jnp.where(hit, weight[:, None, :], 0.0), axis=0)
    hot_weight = jnp.sum(jnp.where(routes_t == busiest, weight, 0.0), axis=0)
    cold = named & (expert_ids != busiest)[:, None]
    slot_of = jnp.where(cold, rank, -1)

    owner = lax.axis_index("expert") == busiest
    own = [w_gate_up[0], down]
    hot_gate_up, hot_down = lax.psum([jnp.where(owner, w, jnp.zeros_like(w)) for w in own], "expert")

    at_slot = slot_of[:, None, :] == jnp.arange(slots, dtype=jnp.int32)[None, :, None]
    pick = at_slot.astype(jnp.bfloat16).reshape(experts * slots, tok_rows)
    outgoing = jnp.dot(pick, tokens, preferred_element_type=jnp.float32).astype(jnp.bfloat16)
    incoming = lax.all_to_all(
        outgoing.reshape(experts, slots, width), "expert", split_axis=0, concat_axis=0, tiled=True
    )
    expert_out = expert_sums(incoming.reshape(experts * slots, width), gate, up, down).astype(
        jnp.bfloat16
    )
    returned = lax.all_to_all(
        expert_out.reshape(experts, slots, width), "expert", split_axis=0, concat_axis=0, tiled=True
    ).reshape(experts * slots, width)

    mix = jnp.where(at_slot, weight_of[:, None, :], 0.0).reshape(experts * slots, tok_rows)
    mix_top = lax.reduce_precision(mix, 8, 7)
    mix_hi = mix_top.astype(jnp.bfloat16)
    mix_lo = (mix - mix_top).astype(jnp.bfloat16)
    both = lax.dot_general(
        jnp.concatenate([mix_hi, mix_lo], axis=1),
        returned,
        (((0,), (0,)), ((), ())),
        preferred_element_type=jnp.float32,
    )
    hot_out = expert_sums(tokens, hot_gate_up[0], hot_gate_up[1], hot_down).astype(jnp.bfloat16)
    mixed = both[:tok_rows] + both[tok_rows:] + hot_weight[:, None] * hot_out.astype(jnp.float32)
    return mixed.astype(jnp.bfloat16)


def solution(mesh):
    return jax.shard_map(
        body,
        mesh=mesh,
        in_specs=(
            P(("dp", "expert"), None),
            P("expert", None, None, None),
            P("expert", None, None),
            P(("dp", "expert"), None),
            P(("dp", "expert"), None),
        ),
        out_specs=P(("dp", "expert"), None),
        check_vma=False,
    )
```

```python
import jax
import jax.numpy as jnp
from jax import lax
from jax.experimental import pallas as pl
from jax.experimental.pallas import tpu as pltpu
from jax.sharding import PartitionSpec as P

SLOTS = 20
GROUP = 4
UNITS = 256


def to_tiles(w):
    rows, cols = w.shape
    return w.reshape(rows // 8, 8, cols // 128, 128).transpose(0, 2, 1, 3).reshape(-1, 8, 128)


def from_tiles(tiles, rows, cols):
    return tiles.reshape(rows // 8, cols // 128, 8, 128).transpose(0, 2, 1, 3).reshape(rows, cols)


def expert_rows(picked, gate, up, down):
    gate_val = jnp.dot(picked, gate, preferred_element_type=jnp.float32)
    up_val = jnp.dot(picked, up, preferred_element_type=jnp.float32)
    hidden = (jax.nn.silu(gate_val) * up_val).astype(jnp.bfloat16)
    return jnp.dot(hidden, down, preferred_element_type=jnp.float32).astype(jnp.bfloat16)


def expert_kernel(x_ref, w_ref, d_ref, o_ref, rows_ref, acc_ref):
    step = pl.program_id(0)
    n, lines, half = x_ref.shape
    units = d_ref.shape[1]

    @pl.when(step == 0)
    def _():
        rows_ref[...] = x_ref[...].astype(jnp.float32).reshape(n * lines, half).astype(jnp.bfloat16)

    def project(which):
        a = jnp.dot(rows_ref[...], w_ref[0, which, :half, :], preferred_element_type=jnp.float32)
        b = jnp.dot(rows_ref[...], w_ref[0, which, half:, :], preferred_element_type=jnp.float32)
        first = lax.broadcasted_iota(jnp.int32, (n, lines, units), 1) < GROUP
        own = jnp.where(first, a.reshape(n, lines, units), b.reshape(n, lines, units))
        return (own + pltpu.roll(own, GROUP, axis=1)).reshape(n * lines, units)

    hidden = (jax.nn.silu(project(0)) * project(1)).astype(jnp.bfloat16)
    left = jnp.dot(hidden, d_ref[0, :, :half], preferred_element_type=jnp.float32)
    right = jnp.dot(hidden, d_ref[0, :, half:], preferred_element_type=jnp.float32)
    first = lax.broadcasted_iota(jnp.int32, (n, lines, half), 1) < GROUP
    part = jnp.where(first, left.reshape(n, lines, half), right.reshape(n, lines, half))

    @pl.when(step == 0)
    def _():
        acc_ref[...] = part

    @pl.when(step > 0)
    def _():
        acc_ref[...] += part

    @pl.when(step == pl.num_programs(0) - 1)
    def _():
        o_ref[...] = acc_ref[...].astype(jnp.bfloat16)


def run_expert(incoming, w_gate_up, w_down):
    sources, lines, half = incoming.shape
    units = w_down.shape[1]
    whole = pl.BlockSpec(incoming.shape, lambda j: (0, 0, 0))
    return pl.pallas_call(
        expert_kernel,
        out_shape=jax.ShapeDtypeStruct(incoming.shape, jnp.bfloat16),
        grid_spec=pltpu.PrefetchScalarGridSpec(
            num_scalar_prefetch=0,
            grid=(units // UNITS,),
            in_specs=[
                whole,
                pl.BlockSpec((1, 2, 2 * half, UNITS), lambda j: (0, 0, 0, j)),
                pl.BlockSpec((1, UNITS, 2 * half), lambda j: (0, j, 0)),
            ],
            out_specs=whole,
            scratch_shapes=[
                pltpu.VMEM((sources * lines, half), jnp.bfloat16),
                pltpu.VMEM((sources, lines, half), jnp.float32),
            ],
        ),
        compiler_params=pltpu.CompilerParams(vmem_limit_bytes=50 << 20),
        cost_estimate=pl.CostEstimate(
            flops=12 * sources * lines * half * units,
            bytes_accessed=4 * sources * lines * half + 12 * half * units,
            transcendentals=0,
        ),
        name="expert_rows",
    )(incoming, w_gate_up, w_down)


def body(tokens, w_gate_up, w_down, routes, gate_scaled):
    experts = lax.axis_size("expert")
    tok_rows, width = tokens.shape
    units = w_down.shape[1]
    half = width // 2
    lines = 2 * GROUP

    routes_t = routes.T
    expert_ids = jnp.arange(experts, dtype=jnp.int32)
    hit = routes_t[:, None, :] == expert_ids[None, :, None]
    named = jnp.any(hit, axis=0)
    earlier = jnp.arange(tok_rows)[:, None] < jnp.arange(tok_rows)[None, :]
    rank = jnp.dot(
        named.astype(jnp.bfloat16), earlier.astype(jnp.bfloat16), preferred_element_type=jnp.float32
    ).astype(jnp.int32)
    counts = jnp.sum(named.astype(jnp.int32), axis=1)
    busiest = jnp.argmax(counts).astype(jnp.int32)
    scaled = gate_scaled.T.astype(jnp.float32)
    weight = scaled / jnp.sum(scaled, axis=0, keepdims=True)
    weight_of = jnp.sum(jnp.where(hit, weight[:, None, :], 0.0), axis=0)
    hot_weight = jnp.sum(jnp.where(routes_t == busiest, weight, 0.0), axis=0)
    cold = named & (expert_ids != busiest)[:, None]
    slot_of = jnp.where(cold, rank, -1)

    owner = lax.axis_index("expert") == busiest
    own = [to_tiles(w_gate_up.reshape(2 * width, units)), to_tiles(w_down[0])]
    own = jnp.concatenate(own, axis=0)
    hot = lax.psum(jnp.where(owner, own, jnp.zeros_like(own)), "expert")
    hot_by_units = from_tiles(hot, 3 * width, units)
    hot_by_width = from_tiles(hot, 3 * units, width)

    stacked = jnp.concatenate([tokens[:, :half], tokens[:, half:]], axis=0)
    line = jnp.arange(lines, dtype=jnp.int32)
    same_side = (line // GROUP)[None, :, None, None] == jnp.arange(2)[None, None, :, None]

    def places(group):
        slot = GROUP * group + line % GROUP
        return (slot_of[:, None, None, :] == slot[None, :, None, None]) & same_side

    def dispatch(group):
        pick = places(group).astype(jnp.bfloat16).reshape(experts * lines, 2 * tok_rows)
        outgoing = jnp.dot(pick, stacked, preferred_element_type=jnp.float32).astype(jnp.bfloat16)
        return lax.all_to_all(
            outgoing.reshape(experts, lines, half), "expert", split_axis=0, concat_axis=0, tiled=True
        )

    def combine(group, returned):
        mix = jnp.where(places(group), weight_of[:, None, None, :], 0.0)
        mix = mix.reshape(experts * lines, 2 * tok_rows)
        mix_top = lax.reduce_precision(mix, 8, 7)
        mix_hi = mix_top.astype(jnp.bfloat16)
        mix_lo = (mix - mix_top).astype(jnp.bfloat16)
        return lax.dot_general(
            jnp.concatenate([mix_hi, mix_lo], axis=1),
            returned.reshape(experts * lines, half),
            (((0,), (0,)), ((), ())),
            preferred_element_type=jnp.float32,
        )

    groups = range(SLOTS // GROUP)
    incoming = [dispatch(g) for g in groups]
    expert_out = [run_expert(x, w_gate_up, w_down) for x in incoming]
    returned = [
        lax.all_to_all(y, "expert", split_axis=0, concat_axis=0, tiled=True) for y in expert_out
    ]
    both = combine(0, returned[0])
    for g in groups[1:]:
        both = both + combine(g, returned[g])
    both = both[: 2 * tok_rows] + both[2 * tok_rows :]
    cold_sum = jnp.concatenate([both[:tok_rows], both[tok_rows:]], axis=1)

    hot_out = expert_rows(
        tokens, hot_by_units[:width], hot_by_units[width : 2 * width], hot_by_width[2 * units :]
    )
    mixed = cold_sum + hot_weight[:, None] * hot_out.astype(jnp.float32)
    return mixed.astype(jnp.bfloat16)


def solution(mesh):
    return jax.shard_map(
        body,
        mesh=mesh,
        in_specs=(
            P(("dp", "expert"), None),
            P("expert", None, None, None),
            P("expert", None, None),
            P(("dp", "expert"), None),
            P(("dp", "expert"), None),
        ),
        out_specs=P(("dp", "expert"), None),
        check_vma=False,
    )
```

```python
import jax
import jax.numpy as jnp
from jax import lax
from jax.experimental import pallas as pl
from jax.experimental.pallas import tpu as pltpu
from jax.sharding import PartitionSpec as P

GROUP = 4
LINES = 2 * GROUP
PARTS = (2, 2, 1)
UNITS = 256
AFTER = 1


def to_tiles(w):
    rows, cols = w.shape
    return w.reshape(rows // 8, 8, cols // 128, 128).transpose(0, 2, 1, 3).reshape(-1, 8, 128)


def from_tiles(tiles, rows, cols):
    return tiles.reshape(rows // 8, cols // 128, 8, 128).transpose(0, 2, 1, 3).reshape(rows, cols)


def expert_rows(picked, gate, up, down):
    gate_val = jnp.dot(picked, gate, preferred_element_type=jnp.float32)
    up_val = jnp.dot(picked, up, preferred_element_type=jnp.float32)
    hidden = (jax.nn.silu(gate_val) * up_val).astype(jnp.bfloat16)
    return jnp.dot(hidden, down, preferred_element_type=jnp.float32).astype(jnp.bfloat16)


def expert_kernel(x_ref, w_ref, d_ref, o_ref, rows_ref, acc_ref):
    step = pl.program_id(0)
    n, lines, half = x_ref.shape
    units = d_ref.shape[1]

    @pl.when(step == 0)
    def _():
        rows_ref[...] = x_ref[...].astype(jnp.float32).reshape(n * lines, half).astype(jnp.bfloat16)

    def project(which):
        a = jnp.dot(rows_ref[...], w_ref[0, which, :half, :], preferred_element_type=jnp.float32)
        b = jnp.dot(rows_ref[...], w_ref[0, which, half:, :], preferred_element_type=jnp.float32)
        first = lax.broadcasted_iota(jnp.int32, (n, lines, units), 1) < GROUP
        own = jnp.where(first, a.reshape(n, lines, units), b.reshape(n, lines, units))
        return (own + pltpu.roll(own, GROUP, axis=1)).reshape(n * lines, units)

    hidden = (jax.nn.silu(project(0)) * project(1)).astype(jnp.bfloat16)
    left = jnp.dot(hidden, d_ref[0, :, :half], preferred_element_type=jnp.float32)
    right = jnp.dot(hidden, d_ref[0, :, half:], preferred_element_type=jnp.float32)
    first = lax.broadcasted_iota(jnp.int32, (n, lines, half), 1) < GROUP
    part = jnp.where(first, left.reshape(n, lines, half), right.reshape(n, lines, half))

    @pl.when(step == 0)
    def _():
        acc_ref[...] = part

    @pl.when(step > 0)
    def _():
        acc_ref[...] += part

    @pl.when(step == pl.num_programs(0) - 1)
    def _():
        o_ref[...] = acc_ref[...].astype(jnp.bfloat16)


def mask_kernel(owner_ref, a_ref, b_ref, o_ref):
    step = pl.program_id(0)
    owner = owner_ref[0] == 1
    in_first = step < pl.num_programs(0) - pl.num_programs(0) // 3

    @pl.when(jnp.logical_and(owner, in_first))
    def _():
        o_ref[...] = a_ref[...]

    @pl.when(jnp.logical_and(owner, jnp.logical_not(in_first)))
    def _():
        o_ref[...] = b_ref[...]

    @pl.when(jnp.logical_not(owner))
    def _():
        o_ref[...] = jnp.zeros_like(o_ref)


def join_if_owner(owner, first, second):
    block = second.shape[0] // 3
    ahead = first.shape[0] // block
    shape = (first.shape[0] + second.shape[0],) + first.shape[1:]
    tile = (block,) + first.shape[1:]
    return pl.pallas_call(
        mask_kernel,
        out_shape=jax.ShapeDtypeStruct(shape, first.dtype),
        grid_spec=pltpu.PrefetchScalarGridSpec(
            num_scalar_prefetch=1,
            grid=(shape[0] // block,),
            in_specs=[
                pl.BlockSpec(tile, lambda i, own: (own[0] * jnp.minimum(i, ahead - 1), 0, 0)),
                pl.BlockSpec(tile, lambda i, own: (own[0] * jnp.maximum(i - ahead, 0), 0, 0)),
            ],
            out_specs=pl.BlockSpec(tile, lambda i, own: (i, 0, 0)),
        ),
        compiler_params=pltpu.CompilerParams(vmem_limit_bytes=20 << 20),
        cost_estimate=pl.CostEstimate(
            flops=0, bytes_accessed=4 * shape[0] * shape[1] * shape[2], transcendentals=0
        ),
        name="join_if_owner",
    )(owner.astype(jnp.int32).reshape(1), first, second)


def run_expert(incoming, chunk, w_gate_up, w_down):
    sources, _, half = incoming.shape
    units = w_down.shape[1]
    shape = (sources, LINES, half)
    return pl.pallas_call(
        expert_kernel,
        out_shape=jax.ShapeDtypeStruct(shape, jnp.bfloat16),
        grid_spec=pltpu.PrefetchScalarGridSpec(
            num_scalar_prefetch=0,
            grid=(units // UNITS,),
            in_specs=[
                pl.BlockSpec(shape, lambda j: (0, chunk, 0)),
                pl.BlockSpec((1, 2, 2 * half, UNITS), lambda j: (0, 0, 0, j)),
                pl.BlockSpec((1, UNITS, 2 * half), lambda j: (0, j, 0)),
            ],
            out_specs=pl.BlockSpec(shape, lambda j: (0, 0, 0)),
            scratch_shapes=[
                pltpu.VMEM((sources * LINES, half), jnp.bfloat16),
                pltpu.VMEM(shape, jnp.float32),
            ],
        ),
        compiler_params=pltpu.CompilerParams(vmem_limit_bytes=50 << 20),
        cost_estimate=pl.CostEstimate(
            flops=12 * sources * LINES * half * units,
            bytes_accessed=4 * sources * LINES * half + 12 * half * units,
            transcendentals=0,
        ),
        name="expert_rows",
    )(incoming, w_gate_up, w_down)


def body(tokens, w_gate_up, w_down, routes, gate_scaled):
    experts = lax.axis_size("expert")
    tok_rows, width = tokens.shape
    units = w_down.shape[1]
    half = width // 2

    routes_t = routes.T
    expert_ids = jnp.arange(experts, dtype=jnp.int32)
    hit = routes_t[:, None, :] == expert_ids[None, :, None]
    named = jnp.any(hit, axis=0)
    earlier = jnp.arange(tok_rows)[:, None] < jnp.arange(tok_rows)[None, :]
    rank = jnp.dot(
        named.astype(jnp.bfloat16), earlier.astype(jnp.bfloat16), preferred_element_type=jnp.float32
    ).astype(jnp.int32)
    counts = jnp.sum(named.astype(jnp.int32), axis=1)
    busiest = jnp.argmax(counts).astype(jnp.int32)
    scaled = gate_scaled.T.astype(jnp.float32)
    weight = scaled / jnp.sum(scaled, axis=0, keepdims=True)
    weight_of = jnp.sum(jnp.where(hit, weight[:, None, :], 0.0), axis=0)
    hot_weight = jnp.sum(jnp.where(routes_t == busiest, weight, 0.0), axis=0)
    cold = named & (expert_ids != busiest)[:, None]
    slot_of = jnp.where(cold, rank, -1)

    owner = lax.axis_index("expert") == busiest
    masked = join_if_owner(owner, to_tiles(w_gate_up.reshape(2 * width, units)), to_tiles(w_down[0]))

    stacked = jnp.concatenate([tokens[:, :half], tokens[:, half:]], axis=0)

    def places(first, count):
        line = jnp.arange(count * LINES, dtype=jnp.int32)
        side = line % LINES // GROUP
        slot = GROUP * (first + line // LINES) + line % GROUP
        same_side = side[None, :, None, None] == jnp.arange(2)[None, None, :, None]
        return (slot_of[:, None, None, :] == slot[None, :, None, None]) & same_side

    def exchange(buffer):
        return lax.all_to_all(buffer, "expert", split_axis=0, concat_axis=0, tiled=True)

    def dispatch(first, count):
        pick = places(first, count).astype(jnp.bfloat16).reshape(-1, 2 * tok_rows)
        outgoing = jnp.dot(pick, stacked, preferred_element_type=jnp.float32).astype(jnp.bfloat16)
        return outgoing.reshape(experts, count * LINES, half)

    def combine(first, count, returned):
        mix = jnp.where(places(first, count), weight_of[:, None, None, :], 0.0)
        mix = mix.reshape(-1, 2 * tok_rows)
        mix_top = lax.reduce_precision(mix, 8, 7)
        mix_hi = mix_top.astype(jnp.bfloat16)
        mix_lo = (mix - mix_top).astype(jnp.bfloat16)
        return lax.dot_general(
            jnp.concatenate([mix_hi, mix_lo], axis=1),
            returned.reshape(-1, half),
            (((0,), (0,)), ((), ())),
            preferred_element_type=jnp.float32,
        )

    spans = [(sum(PARTS[:i]), count) for i, count in enumerate(PARTS)]
    outgoing = [dispatch(*span) for span in spans]
    masked, outgoing[AFTER] = lax.optimization_barrier((masked, outgoing[AFTER]))
    hot = lax.psum(masked, "expert")
    incoming = [exchange(x) for x in outgoing]
    expert_out = [
        run_expert(x, chunk, w_gate_up, w_down)
        for x, count in zip(incoming, PARTS)
        for chunk in range(count)
    ]
    returned = [exchange(y) for y in expert_out]
    both = combine(0, 1, returned[0])
    for chunk, rows in enumerate(returned[1:], 1):
        both = both + combine(chunk, 1, rows)
    both = both[: 2 * tok_rows] + both[2 * tok_rows :]
    cold_sum = jnp.concatenate([both[:tok_rows], both[tok_rows:]], axis=1)

    cold_sum, hot = lax.optimization_barrier((cold_sum, hot))
    hot_by_units = from_tiles(hot, 3 * width, units)
    hot_by_width = from_tiles(hot, 3 * units, width)
    hot_out = expert_rows(
        tokens, hot_by_units[:width], hot_by_units[width : 2 * width], hot_by_width[2 * units :]
    )
    mixed = cold_sum + hot_weight[:, None] * hot_out.astype(jnp.float32)
    return mixed.astype(jnp.bfloat16)


def solution(mesh):
    return jax.shard_map(
        body,
        mesh=mesh,
        in_specs=(
            P(("dp", "expert"), None),
            P("expert", None, None, None),
            P("expert", None, None),
            P(("dp", "expert"), None),
            P(("dp", "expert"), None),
        ),
        out_specs=P(("dp", "expert"), None),
        check_vma=False,
    )
```
